32 devices in a mesh: groups: 2 (over y), replica: 4 (over z), tensor: 4 (over x, core).
Axes of the slice: x: 2, y: 2, z: 4, core: 2. Of those that a mesh axis runs over, the one named last changes fastest.
Arguments:
- queries: bfloat16 [144, 8192], P(('groups', 'replica'), 'tensor'), parts along dimension 0, may hold values from -64 to 64
- past_cache: bfloat16 [2, 144, 128, 1024], P(None, ('groups', 'replica'), None, 'tensor'), parts along dimension 1, may hold values from -6 to 6
- lengths: int32 [144], P(('groups', 'replica')), parts along dimension 0, may hold values from 2 to 128, as said below
- live_counts: int32 [8], P(('groups', 'replica')), parts along dimension 0, may hold values from 1 to 16, as said below
- adapter_index: int32 [144], P(('groups', 'replica')), parts along dimension 0, may hold values from 0 to 15, as said below
- adapter_down: bfloat16 [16, 16, 8192], P('replica', None, 'tensor'), may hold values from -0.0625 to 0.0625
- adapter_up: bfloat16 [16, 16, 8192], P('replica', None, 'tensor'), may hold values from -6 to 6
Outputs:
- attention: bfloat16 [144, 8192], P(('groups', 'replica'), 'tensor'), parts along dimension 0
- adapted: bfloat16 [144, 8192], P(('groups', 'replica'), 'tensor'), parts along dimension 0
The draws below stay inside these ranges and needn't reach their ends.
There are 2 independent parts, one for each index of `groups`. The reference program is written for one: setup_inputs(seed, part) draws one part's arguments, and reference() takes and returns one part's arrays. A program takes and returns all parts, laid end to end along the dimension named above; an argument that names none is the same for every part. Nothing has to cross between parts.
Inputs may be any that keep to these rules, and one draw needn't show every extreme that they name: `adapter_index`: over the first 16 slots of all replicas, exactly 4 distinct adapters appear, homed on 4 distinct replicas. Each of the last 2 slots of a replica names an adapter outside that set; the homes (adapter a lives on replica a // 4) of one replica's last 2 slots are distinct, and some replica is the home of one such slot of every replica. `lengths`: some request has exactly 128. `live_counts`: some replica has exactly 16.
All inputs are finite; a program needn't handle non-finite values.
Results may differ from the reference program's by a relative error of at most 0.008.
Values may be sent and summed in bfloat16 or wider, within the bound.
A program may use at most 64 MiB of HBM per device.

```python
import math
import jax
import jax.numpy as jnp
from jax import lax

D = 8192
HEADS = 64
KV_HEADS = 8
HEAD_DIM = 128
RANK = 16
ADP_DEV = 4
STAY = 16
CONTEXT = 128
HOT = 4
MIG = 2
B_DEV = 18
ADAPTERS = 16
REQUESTS = 72
N_REPLICA = 4


def routing(key):
    base = jax.random.fold_in(key, 11)
    streams = jax.random.split(base, 8)
    replicas = N_REPLICA
    lower_half = replicas // 2
    hot_homes = jax.random.permutation(streams[0], replicas)[:HOT].astype(jnp.int32)
    hot_local = jax.random.randint(streams[1], (HOT,), 0, ADP_DEV, dtype=jnp.int32)
    hot_ids = hot_homes * ADP_DEV + hot_local
    marks = jnp.full((replicas,), -1, jnp.int32).at[hot_homes].set(hot_local)
    picks = jax.random.randint(streams[2], (replicas, STAY), 0, HOT, dtype=jnp.int32)
    lower_picks = jax.random.randint(jax.random.fold_in(base, 101), (replicas, STAY), 1, HOT, dtype=jnp.int32)
    row_ids = jnp.arange(replicas, dtype=jnp.int32)
    picks = jnp.where((row_ids < lower_half)[:, None], lower_picks, picks)
    stay_ids = hot_ids[picks]
    first_row = jax.random.randint(streams[3], (), lower_half, replicas, dtype=jnp.int32)
    stay_ids = stay_ids.at[first_row, :HOT].set(hot_ids)
    full_home = jax.random.randint(streams[4], (), 0, replicas, dtype=jnp.int32)

    def choose(row_key):
        order = jax.random.permutation(row_key, replicas).astype(jnp.int32)[:MIG]
        present = jnp.any(order == full_home)
        return jnp.where(present, order, order.at[MIG - 1].set(full_home))
    targets = jax.vmap(choose)(jax.random.split(streams[5], replicas))
    spare = jax.random.randint(streams[6], (replicas, MIG), 0, ADP_DEV - 1, dtype=jnp.int32)
    loose = jax.random.randint(streams[7], (replicas, MIG), 0, ADP_DEV, dtype=jnp.int32)
    marked = marks[targets]
    local = jnp.where(marked < 0, loose, spare + (spare >= marked).astype(jnp.int32))
    moved_ids = targets * ADP_DEV + local
    return jnp.concatenate([stay_ids, moved_ids], axis=1).reshape(REQUESTS)


def draw_adapter_index(key, part):
    return routing(key)


def draw_lengths(key, part):
    base = jax.random.fold_in(key, 23)
    values = jax.random.randint(base, (REQUESTS,), 2, CONTEXT + 1, dtype=jnp.int32)
    position = jax.random.randint(jax.random.fold_in(base, 1), (), 0, REQUESTS, dtype=jnp.int32)
    return values.at[position].set(CONTEXT)


def draw_live_counts(key, part):
    base = jax.random.fold_in(key, 29)
    values = jax.random.randint(base, (N_REPLICA,), 1, STAY + 1, dtype=jnp.int32)
    position = jax.random.randint(jax.random.fold_in(base, 1), (), 0, N_REPLICA, dtype=jnp.int32)
    return values.at[position].set(STAY)


def paired_draws(key):
    base = jax.random.fold_in(key, 37)
    streams = jax.random.split(base, 2)
    width = KV_HEADS * HEAD_DIM
    queries = jax.random.truncated_normal(streams[0], -6.0, 6.0, (REQUESTS, HEADS * HEAD_DIM), jnp.float32)
    cache = jax.random.truncated_normal(streams[1], -6.0, 6.0, (2, REQUESTS, CONTEXT, width), jnp.float32)
    return (queries, cache)


def draw_queries(key, part):
    return paired_draws(key)[0].astype(jnp.bfloat16)


def draw_past_cache(key, part):
    return paired_draws(key)[1].astype(jnp.bfloat16)


def block_scale(rng, dims, cuts, low, top_value):
    gain, own = 1.0, jax.random.fold_in(rng, 6)
    for dim, parts in cuts:
        steps = jnp.exp(jax.random.uniform(jax.random.fold_in(own, dim), (parts,), jnp.float32, low / len(cuts), top_value / len(cuts)))
        gain = gain * jnp.repeat(steps, dims[dim] // parts).reshape([-1 if axis == dim else 1 for axis in range(len(dims))])
    return gain


def noise(key, extent, spread, limit, shards=(), kind=jnp.bfloat16):
    entries = spread * jax.random.normal(key, extent, jnp.float32)
    if shards:
        entries = entries * block_scale(key, extent, shards, -0.22, 0.18)
    return jnp.clip(entries, -limit, limit).astype(kind)


def setup_inputs(seed: int = 0, part: int = 0) -> dict:
    key_list = jax.random.split(jax.random.key(seed), 8)
    part_splits = jax.random.split(jax.random.fold_in(key_list[7], part), 8)
    queries = draw_queries(jax.random.fold_in(jax.random.fold_in(key_list[7], part), 71), part)
    past_cache = draw_past_cache(jax.random.fold_in(jax.random.fold_in(key_list[7], part), 71), part)
    lengths = draw_lengths(jax.random.fold_in(jax.random.fold_in(key_list[7], part), 71), part)
    live_counts = draw_live_counts(jax.random.fold_in(jax.random.fold_in(key_list[7], part), 71), part)
    adapter_index = draw_adapter_index(jax.random.fold_in(jax.random.fold_in(key_list[7], part), 71), part)
    adapter_down = noise(key_list[5], (ADAPTERS, RANK, HEADS * HEAD_DIM), (HEADS * HEAD_DIM) ** -0.5, 0.0625, ((0, 4), (2, 4)))
    adapter_up = noise(key_list[6], (ADAPTERS, RANK, D), 1.0, 6.0, ((0, 4), (2, 4)))
    return dict(queries=queries, past_cache=past_cache, lengths=lengths, live_counts=live_counts, adapter_index=adapter_index, adapter_down=adapter_down, adapter_up=adapter_up)


SCALING = 2.0

def attend_block(queries, keys, values, visible):
    count = queries.shape[0]
    key_width = keys.shape[-1]
    key_heads = key_width // HEAD_DIM
    group_size = queries.shape[1] // key_width
    context = keys.shape[1]
    query_rows = queries.astype(jnp.float32).reshape(count, key_heads, group_size, HEAD_DIM)
    key_rows = keys.astype(jnp.float32).reshape(count, context, key_heads, HEAD_DIM)
    value_rows = values.astype(jnp.float32).reshape(count, context, key_heads, HEAD_DIM)
    scores = jnp.einsum('nhgd,nlhd->nhgl', query_rows, key_rows) / math.sqrt(HEAD_DIM)
    scores = jnp.where(visible[:, None, None, :], scores, -jnp.inf)
    peak = lax.optimization_barrier(jnp.max(scores, axis=-1, keepdims=True))
    raised = jnp.exp(scores - peak)
    weights = (raised / lax.optimization_barrier(jnp.sum(raised, axis=-1, keepdims=True))).astype(jnp.bfloat16)
    mixed = jnp.einsum('nhgl,nlhd->nhgd', weights.astype(jnp.float32), value_rows)
    return mixed.reshape(count, key_heads * group_size * HEAD_DIM)

def reference(queries, past_cache, lengths, live_counts, adapter_index, adapter_down, adapter_up):
    requests = queries.shape[0]
    blocks = requests // B_DEV
    width = past_cache.shape[-1]
    slot_index = jnp.arange(requests, dtype=jnp.int32) % B_DEV
    owner = jnp.arange(requests, dtype=jnp.int32) // B_DEV
    alive = (slot_index >= STAY) | (slot_index < live_counts[owner])
    position = jnp.arange(CONTEXT, dtype=jnp.int32)
    zero = jnp.zeros((), jnp.int32)

    def one_block(block):
        start = (block * B_DEV).astype(jnp.int32)
        block_queries = lax.dynamic_slice_in_dim(queries, start, B_DEV, 0)
        block_cache = lax.dynamic_slice(past_cache, (zero, start, zero, zero), (2, B_DEV, CONTEXT, width))
        block_lengths = lax.dynamic_slice_in_dim(lengths, start, B_DEV, 0)
        block_alive = lax.dynamic_slice_in_dim(alive, start, B_DEV, 0)
        visible = position[None, :] < block_lengths[:, None]
        mixed = attend_block(block_queries, block_cache[0], block_cache[1], visible)
        attention = jnp.where(block_alive[:, None], mixed, 0.0).astype(jnp.bfloat16)
        chosen = lax.dynamic_slice_in_dim(adapter_index, start, B_DEV, 0)
        down_rows = adapter_down[chosen].astype(jnp.float32)
        up_rows = adapter_up[chosen].astype(jnp.float32)
        rank_rows = jnp.einsum('nc,nrc->nr', attention.astype(jnp.float32), down_rows)
        adapted = (SCALING * jnp.einsum('nr,nrc->nc', rank_rows, up_rows)).astype(jnp.bfloat16)
        return (attention, adapted)
    attention, adapted = lax.map(one_block, jnp.arange(blocks, dtype=jnp.int32))
    return (attention.reshape(requests, -1), adapted.reshape(requests, -1))
```

```python
import functools
import math

import jax
import jax.numpy as jnp
from jax import lax
from jax.experimental import pallas as pl
from jax.experimental.pallas import tpu as pltpu
from jax.sharding import PartitionSpec as P

HEAD_DIM = 128
STAY = 16
SCALING = 2.0
GROUP = 8
EARLY = 1
LIMIT = 67043328 - 240 * 1024
MESH = pl.DeviceIdType.MESH
F32 = jnp.float32
BF16 = jnp.bfloat16


def dot_nt(a, b):
    return lax.dot_general(a, b, (((1,), (1,)), ((), ())), preferred_element_type=F32)


def dot_nn(a, b):
    return lax.dot_general(a, b, (((1,), (0,)), ((), ())), preferred_element_type=F32)


def widen(ranks, up):
    high = ranks.astype(BF16)
    low = (ranks - high.astype(F32)).astype(BF16)
    return SCALING * (dot_nn(high, up) + dot_nn(low, up))


def kernel(
    replicas, tensors,
    lengths_in, live_in, index_in, queries, cache, down, up,
    attention, adapted,
    lengths, live, index, hot, q_in, kv, down_v, up_v, q_rows, o_rows,
    row_out, row_in, row_send, row_back, out_down, hot_down, hot_up, stay_out, stay_in, rank_m, rank_s, rank_e,
    local_sem, group_sem,
    idx_s, idx_r, row_s, row_r, back_s, back_r, hd_s, hd_r, hu_s, hu_r, tm_s, tm_r, ts_s, ts_r, te_s, st_s, st_r,
):
    me = lax.axis_index("replica")
    mine = lax.axis_index("tensor")
    slots, cols = queries.shape
    moving = slots - STAY
    context = cache.shape[2]
    key_heads = cache.shape[3] // HEAD_DIM
    heads = cols // HEAD_DIM
    size = heads // key_heads
    count, rank = down.shape[0], down.shape[1]
    groups = STAY // GROUP
    last = replicas - 1
    edge = (me == 0) | (me == last)
    inner = jnp.logical_not(edge)
    proxy = (me == 1) | (me == last - 1)
    helper = jnp.where(me == 0, 1, last - 1)
    served = jnp.where(me == 1, 0, last)

    def peer(offset):
        return {"replica": lax.rem(me + offset, replicas)}

    def side(offset):
        return {"tensor": lax.rem(mine + offset, tensors)}

    barrier = pltpu.get_barrier_semaphore()
    for d in range(1, replicas):
        pl.semaphore_signal(barrier, inc=1, device_id=peer(d), device_id_type=MESH)
    for d in range(1, tensors):
        pl.semaphore_signal(barrier, inc=1, device_id=side(d), device_id_type=MESH)

    @pl.when(edge)
    def _():
        for d in range(1, tensors):
            pl.semaphore_signal(
                barrier, inc=1, device_id={"replica": helper, **side(d)}, device_id_type=MESH
            )

    load_i = pltpu.make_async_copy(index_in, index.at[0], local_sem.at[0])
    load_n = pltpu.make_async_copy(lengths_in, lengths, local_sem.at[1])
    load_l = pltpu.make_async_copy(live_in, live, local_sem.at[2])
    load_q = pltpu.make_async_copy(queries, q_in, local_sem.at[3])
    load_m = pltpu.make_async_copy(
        cache.at[:, pl.ds(STAY, moving)], kv.at[:, pl.ds(STAY, moving)], local_sem.at[4]
    )
    load_d = pltpu.make_async_copy(down, down_v, local_sem.at[5])
    load_u = pltpu.make_async_copy(up, up_v, local_sem.at[6])
    loads = [
        pltpu.make_async_copy(
            cache.at[:, pl.ds(g * GROUP, GROUP)], kv.at[:, pl.ds(g * GROUP, GROUP)], group_sem.at[g]
        )
        for g in range(groups)
    ]
    load_q.start()
    load_m.start()
    load_i.start()
    load_n.start()
    load_l.start()
    for copy in loads[:2]:
        copy.start()
    load_d.start()
    load_u.start()
    for copy in loads[2:]:
        copy.start()

    def to_peers(source, target, send, recv):
        return [
            pltpu.make_async_remote_copy(
                src_ref=source(d), dst_ref=target.at[d], send_sem=send.at[d - 1],
                recv_sem=recv.at[d - 1], device_id=peer(d), device_id_type=MESH,
            )
            for d in range(1, replicas)
        ]

    def to_sides(buffer, send, recv):
        return [
            pltpu.make_async_remote_copy(
                src_ref=buffer.at[0], dst_ref=buffer.at[d], send_sem=send.at[d - 1],
                recv_sem=recv.at[d - 1], device_id=side(d), device_id_type=MESH,
            )
            for d in range(1, tensors)
        ]

    send_idx = to_peers(lambda d: index.at[0], index, idx_s, idx_r)
    send_rows = to_peers(lambda d: row_out.at[d], row_in, row_s, row_r)
    send_back = [
        pltpu.make_async_remote_copy(
            src_ref=row_send.at[d], dst_ref=row_back.at[d], send_sem=back_s.at[d - 1],
            recv_sem=back_r.at[d - 1], device_id=peer(replicas - d), device_id_type=MESH,
        )
        for d in range(1, replicas)
    ]
    send_tm = to_sides(rank_m, tm_s, tm_r)
    send_ts = [
        pltpu.make_async_remote_copy(
            src_ref=rank_s.at[0], dst_ref=rank_s.at[d], send_sem=ts_s.at[d],
            recv_sem=ts_r.at[d], device_id=side(d), device_id_type=MESH,
        )
        for d in range(1, tensors)
    ]
    send_te = [
        pltpu.make_async_remote_copy(
            src_ref=rank_e, dst_ref=rank_s.at[d], send_sem=te_s.at[d],
            recv_sem=ts_r.at[d], device_id={"replica": served, **side(d)}, device_id_type=MESH,
        )
        for d in range(tensors)
    ]
    send_stay = pltpu.make_async_remote_copy(
        src_ref=stay_out, dst_ref=stay_in, send_sem=st_s, recv_sem=st_r,
        device_id={"replica": helper}, device_id_type=MESH,
    )
    send_hu = to_peers(lambda d: hot_up.at[0], hot_up, hu_s, hu_r)

    def down_to(d, k):
        return pltpu.make_async_remote_copy(
            src_ref=out_down.at[k - 1], dst_ref=hot_down.at[d], send_sem=hd_s.at[d - 1],
            recv_sem=hd_r.at[d - 1], device_id=peer(d), device_id_type=MESH,
        )

    def at_end(d):
        target = lax.rem(me + d, replicas)
        return (target == 0) | (target == last)

    def start_if(flag, copy):
        @pl.when(flag)
        def _():
            copy.start()

    def sent_if(flag, copy):
        @pl.when(flag)
        def _():
            copy.wait_send()

    load_q.wait()
    for h in range(heads):
        q_rows[pl.ds(h, slots, stride=heads), :] = q_in[:, h * HEAD_DIM:(h + 1) * HEAD_DIM].astype(F32)

    head_row = lax.broadcasted_iota(jnp.int32, (heads, 1), 0) // size
    position = lax.broadcasted_iota(jnp.int32, (1, context), 1)
    scale = 1.0 / math.sqrt(HEAD_DIM)

    def attend(requests):
        requests = list(requests)
        scores = []
        for n in requests:
            q = q_rows[n * heads:(n + 1) * heads, :]
            wide = jnp.concatenate(
                [jnp.where(head_row == g, q, 0.0) for g in range(key_heads)], axis=1
            ).astype(BF16)
            scores.append(jnp.where(position < lengths[n], dot_nt(wide, kv[0, n]) * scale, -jnp.inf))
        scores = jnp.concatenate(scores, axis=0)
        peak = jnp.max(scores, axis=-1, keepdims=True)
        raised = jnp.exp(scores - peak)
        weights = (raised / jnp.sum(raised, axis=-1, keepdims=True)).astype(BF16)
        for i, n in enumerate(requests):
            mixed = dot_nn(weights[i * heads:(i + 1) * heads, :], kv[1, n])
            out = mixed[:, :HEAD_DIM]
            for g in range(1, key_heads):
                out = jnp.where(head_row == g, mixed[:, g * HEAD_DIM:(g + 1) * HEAD_DIM], out)
            o_rows[n * heads:(n + 1) * heads, :] = out

    def gather_rows(first, number):
        return jnp.concatenate(
            [o_rows[pl.ds(first * heads + h, number, stride=heads), :] for h in range(heads)], axis=1
        )

    load_i.wait()
    load_n.wait()
    load_l.wait()
    stay_row = lax.broadcasted_iota(jnp.int32, (STAY, 1), 0)
    stay_home = jnp.zeros((STAY, 1), jnp.int32)
    for i in range(STAY):
        stay_home = jnp.where(stay_row == i, index[0, i] // count, stay_home)
    move_rel = [lax.rem(index[0, STAY + j] // count - me + replicas, replicas) for j in range(moving)]

    load_m.wait()
    attend(range(STAY, slots))
    moved = gather_rows(STAY, moving).astype(BF16)
    attention[STAY:slots, :] = moved
    moved = moved.astype(F32)
    replica_row = lax.broadcasted_iota(jnp.int32, (replicas, 1), 0)
    picked = jnp.zeros((replicas, cols), F32)
    for j in range(moving):
        picked = jnp.where(replica_row == move_rel[j], moved[j:j + 1, :], picked)
    row_in[0] = picked[0:1, :]
    for d in range(1, replicas):
        row_out[d] = picked[d:d + 1, :]

    def homed(slot, slot_range):
        best = jnp.int32(-1)
        for i in slot_range:
            local = index[slot, i] - me * count
            best = jnp.maximum(best, jnp.where((local >= 0) & (local < count), local, -1))
        return best

    def attend_group(g):
        loads[g].wait()
        attend(range(g * GROUP, (g + 1) * GROUP))

    def stage(k):
        for slot, flag in ((k, me >= k), (replicas - k, me + k <= last)):
            @pl.when(flag)
            def _():
                send_idx[slot - 1].wait_recv()
                hot[0] = jnp.maximum(hot[0], homed(slot, range(STAY)))
        out_down[k - 1] = down_v[jnp.maximum(hot[0], 0)]
        start_if(me + k < last - 1, down_to(k, k))
        start_if(me - k > 1, down_to(replicas - k, k))
        if k > 1:
            start_if(me + k == last, down_to(k - 1, k))
            start_if(me == k, down_to(replicas - k + 1, k))

    for g in range(EARLY):
        attend_group(g)
    pl.semaphore_wait(barrier, replicas - 1 + tensors - 1 + jnp.where(proxy, tensors - 1, 0))

    for copy in send_idx:
        copy.start()
    for copy in send_rows:
        copy.start()
    hot[0] = homed(0, range(STAY))
    for g in range(EARLY, groups):
        attend_group(g)
    stay = jnp.where(stay_row < live[0], gather_rows(0, STAY), 0.0).astype(BF16)
    attention[0:STAY, :] = stay
    stay_out[...] = stay
    start_if(edge, send_stay)
    load_d.wait()
    load_u.wait()
    for k in range(1, replicas):
        stage(k)
    chosen = jnp.maximum(hot[0], 0)
    hot_down[0] = down_v[chosen]
    hot_up[0] = up_v[chosen]

    asked = jnp.full((replicas, 1), -1, jnp.int32)
    for d in range(replicas):
        asked = jnp.where(replica_row == d, homed(d, range(STAY, slots)), asked)
    for copy in send_rows:
        copy.wait_recv()
    rows = jnp.concatenate([row_in[d] for d in range(replicas)], axis=0).astype(BF16)
    partial = dot_nt(rows, down_v[...].reshape(count * rank, cols))
    owner = lax.broadcasted_iota(jnp.int32, partial.shape, 1) // rank
    rank_m[0] = jnp.where(owner == asked, partial, 0.0)
    for copy in send_tm:
        copy.start()

    for d in range(1, replicas):
        start_if(at_end(d), send_hu[d - 1])

    for copy in send_tm:
        copy.wait_recv()
    total = rank_m[0]
    for d in range(1, tensors):
        total = total + rank_m[d]
    made = widen(total, up_v[...].reshape(count * rank, cols)).astype(BF16).astype(F32)
    row_back[0] = made[0:1, :]
    for d in range(1, replicas):
        row_send[d] = made[d:d + 1, :]
    for copy in send_back:
        copy.start()
    for d in range(1, replicas):
        start_if(jnp.logical_not(at_end(d)), send_hu[d - 1])

    def by_home(buffer):
        return jnp.concatenate([buffer[lax.rem(me - h + replicas, replicas)] for h in range(replicas)], axis=0)

    def ranks(rows, home):
        partial = dot_nt(rows, by_home(hot_down))
        owner = lax.broadcasted_iota(jnp.int32, partial.shape, 1) // rank
        return jnp.where(owner == home, partial, 0.0)

    @pl.when(inner)
    def _():
        for d in range(1, replicas):
            down_to(d, 1).wait_recv()

    @pl.when(proxy)
    def _():
        send_stay.wait_recv()
        slot = jnp.where(me == 1, 1, last)
        home = jnp.zeros((STAY, 1), jnp.int32)
        for i in range(STAY):
            home = jnp.where(stay_row == i, index[slot, i] // count, home)
        rank_e[...] = ranks(stay_in[...], home)
        for copy in send_te:
            copy.start()

    @pl.when(inner)
    def _():
        rank_s[0] = ranks(stay_out[...], stay_home)
        for copy in send_ts:
            copy.start()

    for copy in send_back:
        copy.wait_recv()
    back = jnp.concatenate([row_back[d] for d in range(replicas)], axis=0)
    adapted[STAY:slots, :] = jnp.concatenate(
        [
            jnp.sum(jnp.where(replica_row == move_rel[j], back, 0.0), axis=0, keepdims=True)
            for j in range(moving)
        ],
        axis=0,
    ).astype(BF16)

    for copy in send_ts:
        copy.wait_recv()

    @pl.when(edge)
    def _():
        send_te[0].wait_recv()

    total = rank_s[0]
    for d in range(1, tensors):
        total = total + rank_s[d]
    for copy in send_hu:
        copy.wait_recv()
    adapted[0:STAY, :] = widen(total, by_home(hot_up)).astype(BF16)

    for copy in send_idx + send_rows + send_back + send_tm + send_hu:
        copy.wait_send()
    sent_if(edge, send_stay)
    for copy in send_ts:
        sent_if(inner, copy)
    for copy in send_te:
        sent_if(proxy, copy)
    for d in range(1, replicas):
        sent_if(jnp.logical_not(at_end(d)), down_to(d, 1))


def hand_over(attention, adapted, attention_out, adapted_out, sem):
    first = pltpu.make_async_copy(attention, attention_out, sem.at[0])
    second = pltpu.make_async_copy(adapted, adapted_out, sem.at[1])
    first.start()
    second.start()
    first.wait()
    second.wait()


def on_device(replicas, tensors, queries, past_cache, lengths, live_counts, adapter_index, adapter_down, adapter_up):
    slots, cols = queries.shape
    count, rank = adapter_down.shape[0], adapter_down.shape[1]
    heads = cols // HEAD_DIM
    out = jax.ShapeDtypeStruct((slots, cols), BF16)
    held = pltpu.VMEM((slots, cols), BF16)
    anywhere = pl.BlockSpec(memory_space=pl.ANY)
    vmem = pl.BlockSpec(memory_space=pltpu.VMEM)
    dma = pltpu.SemaphoreType.DMA
    rep = dma((max(replicas - 1, 1),))
    ten = dma((max(tensors - 1, 1),))
    all_ten = dma((tensors,))
    scratch = [
        pltpu.SMEM((slots,), jnp.int32),
        pltpu.SMEM((1,), jnp.int32),
        pltpu.SMEM((replicas, slots), jnp.int32),
        pltpu.SMEM((1,), jnp.int32),
        pltpu.VMEM((slots, cols), BF16),
        pltpu.VMEM(past_cache.shape, BF16),
        pltpu.VMEM(adapter_down.shape, BF16),
        pltpu.VMEM(adapter_up.shape, BF16),
        pltpu.VMEM((slots * heads, HEAD_DIM), F32),
        pltpu.VMEM((slots * heads, HEAD_DIM), F32),
        pltpu.VMEM((replicas, 1, cols), F32),
        pltpu.VMEM((replicas, 1, cols), F32),
        pltpu.VMEM((replicas, 1, cols), F32),
        pltpu.VMEM((replicas, 1, cols), F32),
        pltpu.VMEM((replicas - 1, rank, cols), BF16),
        pltpu.VMEM((replicas, rank, cols), BF16),
        pltpu.VMEM((replicas, rank, cols), BF16),
        pltpu.VMEM((STAY, cols), BF16),
        pltpu.VMEM((STAY, cols), BF16),
        pltpu.VMEM((tensors, replicas, count * rank), F32),
        pltpu.VMEM((tensors, STAY, replicas * rank), F32),
        pltpu.VMEM((STAY, replicas * rank), F32),
        dma((7,)),
        dma((STAY // GROUP,)),
        rep, rep, rep, rep, rep, rep, rep, rep, rep, rep, ten, ten, all_ten, all_ten, all_ten, dma(()), dma(()),
    ]
    results = pl.pallas_call(
        functools.partial(kernel, replicas, tensors),
        out_shape=(held, held),
        in_specs=[anywhere] * 7,
        out_specs=(vmem, vmem),
        scratch_shapes=scratch,
        compiler_params=pltpu.CompilerParams(collective_id=0, has_side_effects=True, vmem_limit_bytes=LIMIT),
    )(lengths, live_counts, adapter_index, queries, past_cache, adapter_down, adapter_up)
    return pl.pallas_call(
        hand_over,
        out_shape=(out, out),
        in_specs=[vmem, vmem],
        out_specs=(anywhere, anywhere),
        scratch_shapes=[dma((2,))],
        compiler_params=pltpu.CompilerParams(vmem_limit_bytes=4 * 1024 * 1024),
    )(*results)


def solution(mesh):
    in_specs = (
        P(("groups", "replica"), "tensor"),
        P(None, ("groups", "replica"), None, "tensor"),
        P(("groups", "replica")),
        P(("groups", "replica")),
        P(("groups", "replica")),
        P("replica", None, "tensor"),
        P("replica", None, "tensor"),
    )
    out_specs = (P(("groups", "replica"), "tensor"), P(("groups", "replica"), "tensor"))
    body = functools.partial(on_device, mesh.shape["replica"], mesh.shape["tensor"])
    return jax.shard_map(body, mesh=mesh, in_specs=in_specs, out_specs=out_specs, check_vma=False)
```

```python
import functools
import math

import jax
import jax.numpy as jnp
from jax import lax
from jax.experimental import pallas as pl
from jax.experimental.pallas import tpu as pltpu
from jax.sharding import PartitionSpec as P

HEAD_DIM = 128
STAY = 16
SCALING = 2.0
GROUP = 8
EARLY = 1
LIMIT = 67043328 - 240 * 1024
MESH = pl.DeviceIdType.MESH
F32 = jnp.float32
BF16 = jnp.bfloat16


def dot_nt(a, b):
    return lax.dot_general(a, b, (((1,), (1,)), ((), ())), preferred_element_type=F32)


def dot_nn(a, b):
    return lax.dot_general(a, b, (((1,), (0,)), ((), ())), preferred_element_type=F32)


def widen(ranks, up):
    high = ranks.astype(BF16)
    low = (ranks - high.astype(F32)).astype(BF16)
    return SCALING * (dot_nn(high, up) + dot_nn(low, up))


def kernel(
    replicas, tensors,
    lengths_in, live_in, index_in, queries, cache, down, up,
    attention, adapted,
    lengths, live, index, hot, q_in, kv, maps_v, q_rows, o_rows,
    row_out, row_in, row_send, row_back, out_up, hot_down, hot_up, stay_in, rank_m, rank_out, rank_s,
    local_sem, group_sem,
    idx_s, idx_r, row_s, row_r, back_s, back_r, hd_s, hd_r, hu_s, hu_r, tm_s, tm_r, st_s, st_r, rs_s, rs_r,
):
    me = lax.axis_index("replica")
    mine = lax.axis_index("tensor")
    slots, cols = queries.shape
    moving = slots - STAY
    context = cache.shape[2]
    key_heads = cache.shape[3] // HEAD_DIM
    heads = cols // HEAD_DIM
    size = heads // key_heads
    count, rank = down.shape[0], down.shape[1]
    groups = STAY // GROUP
    down_v, up_v = maps_v.at[0], maps_v.at[1]
    last = replicas - 1
    half = replicas // 2
    lower = me < half
    base = jnp.where(lower, 0, half)
    head = jnp.where(lower, half - 1, half)
    leads = me == head

    def peer(offset):
        return {"replica": lax.rem(me + offset, replicas)}

    def side(offset):
        return {"tensor": lax.rem(mine + offset, tensors)}

    barrier = pltpu.get_barrier_semaphore()
    for d in range(1, replicas):
        pl.semaphore_signal(barrier, inc=1, device_id=peer(d), device_id_type=MESH)
    for d in range(1, tensors):
        pl.semaphore_signal(barrier, inc=1, device_id=side(d), device_id_type=MESH)

    for h in (half - 1, half):
        @pl.when(me != h)
        def _():
            for d in range(1, tensors):
                pl.semaphore_signal(barrier, inc=1, device_id={"replica": h, **side(d)}, device_id_type=MESH)

    load_i = pltpu.make_async_copy(index_in, index.at[0], local_sem.at[0])
    load_n = pltpu.make_async_copy(lengths_in, lengths, local_sem.at[1])
    load_l = pltpu.make_async_copy(live_in, live, local_sem.at[2])
    load_q = pltpu.make_async_copy(queries, q_in, local_sem.at[3])
    load_m = pltpu.make_async_copy(
        cache.at[:, pl.ds(STAY, moving)], kv.at[:, pl.ds(STAY, moving)], local_sem.at[4]
    )
    load_d = pltpu.make_async_copy(down, down_v, local_sem.at[5])
    load_u = pltpu.make_async_copy(up, up_v, local_sem.at[6])
    loads = [
        pltpu.make_async_copy(
            cache.at[:, pl.ds(g * GROUP, GROUP)], kv.at[:, pl.ds(g * GROUP, GROUP)], group_sem.at[g]
        )
        for g in range(groups)
    ]
    load_q.start()
    load_m.start()
    load_i.start()
    load_n.start()
    load_l.start()
    for copy in loads[:2]:
        copy.start()
    load_d.start()
    load_u.start()
    for copy in loads[2:]:
        copy.start()

    def to_peers(source, target, send, recv, own=False):
        return [
            pltpu.make_async_remote_copy(
                src_ref=source(d), dst_ref=target.at[d], send_sem=send.at[0],
                recv_sem=recv.at[d - 1 if own else 0], device_id=peer(d), device_id_type=MESH,
            )
            for d in range(1, replicas)
        ]

    def to_sides(buffer, send, recv):
        return [
            pltpu.make_async_remote_copy(
                src_ref=buffer.at[0], dst_ref=buffer.at[d], send_sem=send.at[0],
                recv_sem=recv.at[0], device_id=side(d), device_id_type=MESH,
            )
            for d in range(1, tensors)
        ]

    def drain(ref, sem):
        pltpu.make_async_copy(ref, ref, sem.at[0]).wait()

    send_idx = to_peers(lambda d: index.at[0], index, idx_s, idx_r, own=True)
    send_rows = to_peers(lambda d: row_out.at[d], row_in, row_s, row_r)
    send_back = [
        pltpu.make_async_remote_copy(
            src_ref=row_send.at[d], dst_ref=row_back.at[d], send_sem=back_s.at[0],
            recv_sem=back_r.at[0], device_id=peer(replicas - d), device_id_type=MESH,
        )
        for d in range(1, replicas)
    ]
    send_tm = to_sides(rank_m, tm_s, tm_r)
    def stay_to(h):
        return pltpu.make_async_remote_copy(
            src_ref=stay_in.at[0], dst_ref=stay_in.at[lax.rem(h - me + replicas, replicas)], send_sem=st_s.at[0],
            recv_sem=st_r.at[0], device_id={"replica": h}, device_id_type=MESH,
        )

    send_down = pltpu.make_async_remote_copy(
        src_ref=hot_down.at[me - base], dst_ref=hot_down.at[me - base], send_sem=hd_s.at[0],
        recv_sem=hd_r.at[0], device_id={"replica": head}, device_id_type=MESH,
    )

    def ranks_to(d, t):
        side_slot = jnp.where(lower, 0, tensors) + t
        return pltpu.make_async_remote_copy(
            src_ref=rank_out.at[d], dst_ref=rank_s.at[side_slot], send_sem=rs_s.at[t],
            recv_sem=rs_r.at[0], device_id={"replica": lax.rem(me - d + replicas, replicas), **side(t)},
            device_id_type=MESH,
        )

    def up_to(d, source):
        return pltpu.make_async_remote_copy(
            src_ref=source, dst_ref=hot_up.at[d], send_sem=hu_s.at[0],
            recv_sem=hu_r.at[0], device_id=peer(d), device_id_type=MESH,
        )

    def start_if(flag, copy):
        @pl.when(flag)
        def _():
            copy.start()

    def sent_if(flag, copy):
        @pl.when(flag)
        def _():
            copy.wait_send()

    load_q.wait()
    for h in range(heads):
        q_rows[pl.ds(h, slots, stride=heads), :] = q_in[:, h * HEAD_DIM:(h + 1) * HEAD_DIM].astype(F32)

    head_row = lax.broadcasted_iota(jnp.int32, (heads, 1), 0) // size
    position = lax.broadcasted_iota(jnp.int32, (1, context), 1)
    scale = 1.0 / math.sqrt(HEAD_DIM)

    def attend(requests):
        requests = list(requests)
        scores = []
        for n in requests:
            q = q_rows[n * heads:(n + 1) * heads, :]
            wide = jnp.concatenate(
                [jnp.where(head_row == g, q, 0.0) for g in range(key_heads)], axis=1
            ).astype(BF16)
            scores.append(jnp.where(position < lengths[n], dot_nt(wide, kv[0, n]) * scale, -jnp.inf))
        scores = jnp.concatenate(scores, axis=0)
        peak = jnp.max(scores, axis=-1, keepdims=True)
        raised = jnp.exp(scores - peak)
        weights = (raised / jnp.sum(raised, axis=-1, keepdims=True)).astype(BF16)
        for i, n in enumerate(requests):
            mixed = dot_nn(weights[i * heads:(i + 1) * heads, :], kv[1, n])
            out = mixed[:, :HEAD_DIM]
            for g in range(1, key_heads):
                out = jnp.where(head_row == g, mixed[:, g * HEAD_DIM:(g + 1) * HEAD_DIM], out)
            o_rows[n * heads:(n + 1) * heads, :] = out

    def gather_rows(first, number):
        return jnp.concatenate(
            [o_rows[pl.ds(first * heads + h, number, stride=heads), :] for h in range(heads)], axis=1
        )

    load_i.wait()
    load_n.wait()
    load_l.wait()
    stay_row = lax.broadcasted_iota(jnp.int32, (STAY, 1), 0)
    stay_home = jnp.zeros((STAY, 1), jnp.int32)
    for i in range(STAY):
        stay_home = jnp.where(stay_row == i, index[0, i] // count, stay_home)
    move_rel = [lax.rem(index[0, STAY + j] // count - me + replicas, replicas) for j in range(moving)]

    load_m.wait()
    attend(range(STAY, slots))
    moved = gather_rows(STAY, moving).astype(BF16)
    attention[STAY:slots, :] = moved
    moved = moved.astype(F32)
    replica_row = lax.broadcasted_iota(jnp.int32, (replicas, 1), 0)
    picked = jnp.zeros((replicas, cols), F32)
    for j in range(moving):
        picked = jnp.where(replica_row == move_rel[j], moved[j:j + 1, :], picked)
    row_in[0] = picked[0:1, :]
    for d in range(1, replicas):
        row_out[d] = picked[d:d + 1, :]

    def homed(slot, slot_range):
        best = jnp.int32(-1)
        for i in slot_range:
            local = index[slot, i] - me * count
            best = jnp.maximum(best, jnp.where((local >= 0) & (local < count), local, -1))
        return best

    def attend_group(g):
        loads[g].wait()
        attend(range(g * GROUP, (g + 1) * GROUP))

    def stage(k):
        for slot, flag in ((k, me >= k), (replicas - k, me + k <= last)):
            @pl.when(flag)
            def _():
                send_idx[slot - 1].wait_recv()
                hot[0] = jnp.maximum(hot[0], homed(slot, range(STAY)))
        out_up[k - 1] = up_v[jnp.maximum(hot[0], 0)]
        other = jnp.where(lower, half, half - 1)
        start_if(leads & (me + k <= last) & (me + k != other), up_to(k, out_up.at[k - 1]))
        start_if(leads & (me >= k) & (me - k != other), up_to(replicas - k, out_up.at[k - 1]))

    for g in range(EARLY):
        attend_group(g)
    pl.semaphore_wait(barrier, jnp.where(leads, replicas * tensors - 1, replicas + tensors - 2))

    for copy in send_idx:
        copy.start()
    for copy in send_rows:
        copy.start()
    hot[0] = homed(0, range(STAY))
    for g in range(EARLY, groups):
        attend_group(g)
    stay = jnp.where(stay_row < live[0], gather_rows(0, STAY), 0.0).astype(BF16)
    attention[0:STAY, :] = stay
    stay_in[0] = stay
    for h in (half - 1, half):
        start_if(me != h, stay_to(h))
    load_d.wait()
    load_u.wait()
    for k in range(1, replicas):
        stage(k)
    chosen = jnp.maximum(hot[0], 0)
    hot_down[me - base] = down_v[chosen]
    hot_up[0] = up_v[chosen]
    start_if(jnp.logical_not(leads), send_down)
    for step in range(1, replicas):
        far = replicas - step
        start_if(jnp.logical_not(leads) & lower & (me + far <= last), up_to(far, hot_up.at[0]))
        start_if(jnp.logical_not(leads) & jnp.logical_not(lower) & (me >= far), up_to(replicas - far, hot_up.at[0]))
    for step in range(1, half):
        start_if(jnp.logical_not(leads) & lower & (me >= step), up_to(replicas - step, hot_up.at[0]))
        start_if(jnp.logical_not(leads) & jnp.logical_not(lower) & (me + step <= last), up_to(step, hot_up.at[0]))

    asked = jnp.full((replicas, 1), -1, jnp.int32)
    for d in range(replicas):
        asked = jnp.where(replica_row == d, homed(d, range(STAY, slots)), asked)
    drain(row_in.at[pl.ds(1, last)], row_r)
    rows = jnp.concatenate([row_in[d] for d in range(replicas)], axis=0).astype(BF16)
    partial = dot_nt(rows, down_v[...].reshape(count * rank, cols))
    owner = lax.broadcasted_iota(jnp.int32, partial.shape, 1) // rank
    rank_m[0] = jnp.where(owner == asked, partial, 0.0)
    for copy in send_tm:
        copy.start()

    homes = []
    for d in range(replicas):
        home = jnp.zeros((STAY, 1), jnp.int32)
        for i in range(STAY):
            home = jnp.where(stay_row == i, index[d, i] // count, home)
        homes.append(home)
    homes = jnp.concatenate(homes, axis=0) - base
    drain(rank_m.at[pl.ds(1, tensors - 1)], tm_r)
    total = rank_m[0]
    for d in range(1, tensors):
        total = total + rank_m[d]
    made = widen(total, up_v[...].reshape(count * rank, cols)).astype(BF16).astype(F32)
    row_back[0] = made[0:1, :]
    for d in range(1, replicas):
        row_send[d] = made[d:d + 1, :]
    for copy in send_back:
        copy.start()
    part = half * rank
    lines = STAY // 2

    @pl.when(leads)
    def _():
        drain(stay_in.at[pl.ds(1, last)], st_r)
        if half > 1:
            drain(hot_down.at[pl.ds(1, half - 1)], hd_r)
        partial = dot_nt(stay_in[...].reshape(replicas * STAY, cols), hot_down[...].reshape(part, cols))
        owner = lax.broadcasted_iota(jnp.int32, partial.shape, 1) // rank
        partial = jnp.where(owner == homes, partial, 0.0)
        for d in range(replicas):
            block = partial[d * STAY:(d + 1) * STAY]
            rank_out[d] = jnp.concatenate([block[:lines], block[lines:]], axis=1)
        rank_s[jnp.where(lower, 0, tensors)] = rank_out[0]
        for d in range(replicas):
            for t in range(tensors):
                if d or t:
                    ranks_to(d, t).start()
        start_if(lower, up_to(1, hot_up.at[0]))
        start_if(jnp.logical_not(lower), up_to(last, hot_up.at[0]))

    drain(row_back.at[pl.ds(1, last)], back_r)
    back = jnp.concatenate([row_back[d] for d in range(replicas)], axis=0)
    adapted[STAY:slots, :] = jnp.concatenate(
        [
            jnp.sum(jnp.where(replica_row == move_rel[j], back, 0.0), axis=0, keepdims=True)
            for j in range(moving)
        ],
        axis=0,
    ).astype(BF16)

    @pl.when(leads)
    def _():
        drain(rank_s.at[pl.ds(1, 2 * tensors - 1)], rs_r)

    @pl.when(jnp.logical_not(leads))
    def _():
        drain(rank_s, rs_r)

    totals = []
    for side_slot in (0, tensors):
        total = rank_s[side_slot]
        for d in range(1, tensors):
            total = total + rank_s[side_slot + d]
        totals.append(jnp.concatenate([total[:, :part], total[:, part:]], axis=0))
    total = jnp.concatenate(totals, axis=1)
    drain(hot_up.at[pl.ds(1, last)], hu_r)
    ups = jnp.concatenate([hot_up[lax.rem(me - h + replicas, replicas)] for h in range(replicas)], axis=0)
    adapted[0:STAY, :] = widen(total, ups).astype(BF16)

    drain(index.at[pl.ds(1, last)], idx_s)
    drain(row_out.at[pl.ds(1, last)], row_s)
    drain(row_send.at[pl.ds(1, last)], back_s)
    drain(rank_m.at[pl.ds(1, tensors - 1)], tm_s)
    drain(hot_up.at[pl.ds(1, last)], hu_s)

    @pl.when(leads)
    def _():
        drain(stay_in.at[0], st_s)
        drain(rank_out.at[pl.ds(1, last)], rs_s.at[pl.ds(0, 1)])
        for t in range(1, tensors):
            drain(rank_out, rs_s.at[pl.ds(t, 1)])

    @pl.when(jnp.logical_not(leads))
    def _():
        drain(stay_in.at[pl.ds(0, 2)], st_s)
        drain(hot_down.at[0], hd_s)


def hand_over(attention, adapted, attention_out, adapted_out, sem):
    first = pltpu.make_async_copy(attention, attention_out, sem.at[0])
    second = pltpu.make_async_copy(adapted, adapted_out, sem.at[1])
    first.start()
    second.start()
    first.wait()
    second.wait()


def on_device(replicas, tensors, queries, past_cache, lengths, live_counts, adapter_index, adapter_down, adapter_up):
    slots, cols = queries.shape
    count, rank = adapter_down.shape[0], adapter_down.shape[1]
    heads = cols // HEAD_DIM
    out = jax.ShapeDtypeStruct((slots, cols), BF16)
    held = pltpu.VMEM((slots, cols), BF16)
    anywhere = pl.BlockSpec(memory_space=pl.ANY)
    vmem = pl.BlockSpec(memory_space=pltpu.VMEM)
    dma = pltpu.SemaphoreType.DMA
    rep = dma((replicas - 1,))
    one = dma((1,))
    ten = dma((tensors,))
    half = replicas // 2
    scratch = [
        pltpu.SMEM((slots,), jnp.int32),
        pltpu.SMEM((1,), jnp.int32),
        pltpu.SMEM((replicas, slots), jnp.int32),
        pltpu.SMEM((1,), jnp.int32),
        pltpu.VMEM((slots, cols), BF16),
        pltpu.VMEM(past_cache.shape, BF16),
        pltpu.VMEM((2, *adapter_down.shape), BF16),
        pltpu.VMEM((slots * heads, HEAD_DIM), F32),
        pltpu.VMEM((slots * heads, HEAD_DIM), F32),
        pltpu.VMEM((replicas, 1, cols), F32),
        pltpu.VMEM((replicas, 1, cols), F32),
        pltpu.VMEM((replicas, 1, cols), F32),
        pltpu.VMEM((replicas, 1, cols), F32),
        pltpu.VMEM((replicas - 1, rank, cols), BF16),
        pltpu.VMEM((half, rank, cols), BF16),
        pltpu.VMEM((replicas, rank, cols), BF16),
        pltpu.VMEM((replicas, STAY, cols), BF16),
        pltpu.VMEM((tensors, replicas, count * rank), F32),
        pltpu.VMEM((replicas, STAY // 2, replicas * rank), F32),
        pltpu.VMEM((2 * tensors, STAY // 2, replicas * rank), F32),
        dma((7,)),
        dma((STAY // GROUP,)),
        one, rep, one, one, one, one, one, one, one, one, one, one, one, one, ten, one,
    ]
    results = pl.pallas_call(
        functools.partial(kernel, replicas, tensors),
        out_shape=(held, held),
        in_specs=[anywhere] * 7,
        out_specs=(vmem, vmem),
        scratch_shapes=scratch,
        compiler_params=pltpu.CompilerParams(collective_id=0, has_side_effects=True, vmem_limit_bytes=LIMIT),
    )(lengths, live_counts, adapter_index, queries, past_cache, adapter_down, adapter_up)
    return pl.pallas_call(
        hand_over,
        out_shape=(out, out),
        in_specs=[vmem, vmem],
        out_specs=(anywhere, anywhere),
        scratch_shapes=[dma((2,))],
        compiler_params=pltpu.CompilerParams(vmem_limit_bytes=4 * 1024 * 1024),
    )(*results)


def solution(mesh):
    in_specs = (
        P(("groups", "replica"), "tensor"),
        P(None, ("groups", "replica"), None, "tensor"),
        P(("groups", "replica")),
        P(("groups", "replica")),
        P(("groups", "replica")),
        P("replica", None, "tensor"),
        P("replica", None, "tensor"),
    )
    out_specs = (P(("groups", "replica"), "tensor"), P(("groups", "replica"), "tensor"))
    body = functools.partial(on_device, mesh.shape["replica"], mesh.shape["tensor"])
    return jax.shard_map(body, mesh=mesh, in_specs=in_specs, out_specs=out_specs, check_vma=False)
```

```python
import functools
import math

import jax
import jax.numpy as jnp
from jax import lax
from jax.experimental import pallas as pl
from jax.experimental.pallas import tpu as pltpu
from jax.sharding import PartitionSpec as P

HEAD_DIM = 128
STAY = 16
SCALING = 2.0
GROUP = 8
EARLY = 0
LIMIT = 67043328 - 240 * 1024
MESH = pl.DeviceIdType.MESH
F32 = jnp.float32
BF16 = jnp.bfloat16


def dot_nt(a, b):
    return lax.dot_general(a, b, (((1,), (1,)), ((), ())), preferred_element_type=F32)


def dot_nn(a, b):
    return lax.dot_general(a, b, (((1,), (0,)), ((), ())), preferred_element_type=F32)


def widen(ranks, up):
    high = ranks.astype(BF16)
    low = (ranks - high.astype(F32)).astype(BF16)
    return SCALING * (dot_nn(high, up) + dot_nn(low, up))


def kernel(
    replicas, tensors,
    lengths_in, live_in, index_in, queries, cache, down, up,
    attention, adapted,
    lengths, live, index, hot, q_in, kv, maps_v, q_rows, o_rows,
    row_out, row_in, row_send, row_back, out_up, hot_down, hot_up, stay_in, rank_m, rank_out, rank_s,
    local_sem, group_sem,
    idx_s, idx_r, row_s, row_r, back_s, back_r, hd_s, hd_r, hu_s, hu_r, tm_s, tm_r, st_s, st_r, rs_s, rs_r,
):
    me = lax.axis_index("replica")
    mine = lax.axis_index("tensor")
    slots, cols = queries.shape
    moving = slots - STAY
    context = cache.shape[2]
    key_heads = cache.shape[3] // HEAD_DIM
    heads = cols // HEAD_DIM
    size = heads // key_heads
    count, rank = down.shape[0], down.shape[1]
    groups = STAY // GROUP
    down_v, up_v = maps_v.at[0], maps_v.at[1]
    last = replicas - 1
    half = replicas // 2
    lower = me < half
    base = jnp.where(lower, 0, half)
    head = jnp.where(lower, half - 1, half)
    leads = me == head

    def peer(offset):
        return {"replica": lax.rem(me + offset, replicas)}

    def side(offset):
        return {"tensor": lax.rem(mine + offset, tensors)}

    barrier = pltpu.get_barrier_semaphore()
    for d in range(1, replicas):
        pl.semaphore_signal(barrier, inc=1, device_id=peer(d), device_id_type=MESH)
    for d in range(1, tensors):
        pl.semaphore_signal(barrier, inc=1, device_id=side(d), device_id_type=MESH)

    odd = lax.rem(mine, 2) == 1

    @pl.when(jnp.logical_not(odd))
    def _():
        for d in range(1, replicas):
            pl.semaphore_signal(
                barrier, inc=1, device_id={**peer(d), "tensor": mine + 1}, device_id_type=MESH
            )

    load_i = pltpu.make_async_copy(index_in, index.at[0], local_sem.at[0])
    load_n = pltpu.make_async_copy(lengths_in, lengths, local_sem.at[1])
    load_l = pltpu.make_async_copy(live_in, live, local_sem.at[2])
    load_q = pltpu.make_async_copy(queries, q_in, local_sem.at[3])
    load_m = pltpu.make_async_copy(
        cache.at[:, pl.ds(STAY, moving)], kv.at[:, pl.ds(STAY, moving)], local_sem.at[4]
    )
    load_d = pltpu.make_async_copy(down, down_v, local_sem.at[5])
    load_u = pltpu.make_async_copy(up, up_v, local_sem.at[6])
    loads = [
        pltpu.make_async_copy(
            cache.at[:, pl.ds(g * GROUP, GROUP)], kv.at[:, pl.ds(g * GROUP, GROUP)], group_sem.at[g]
        )
        for g in range(groups)
    ]
    load_q.start()
    load_m.start()
    load_i.start()
    load_n.start()
    load_l.start()
    for copy in loads[:2]:
        copy.start()
    load_d.start()
    load_u.start()
    for copy in loads[2:]:
        copy.start()

    def to_peers(source, target, send, recv):
        return [
            pltpu.make_async_remote_copy(
                src_ref=source(d), dst_ref=target.at[d], send_sem=send.at[0],
                recv_sem=recv.at[0], device_id=peer(d), device_id_type=MESH,
            )
            for d in range(1, replicas)
        ]

    def to_sides(buffer, send, recv):
        return [
            pltpu.make_async_remote_copy(
                src_ref=buffer.at[0], dst_ref=buffer.at[d], send_sem=send.at[0],
                recv_sem=recv.at[0], device_id=side(d), device_id_type=MESH,
            )
            for d in range(1, tensors)
        ]

    def drain(ref, sem):
        pltpu.make_async_copy(ref, ref, sem.at[0]).wait()

    def index_to(d, back):
        return pltpu.make_async_remote_copy(
            src_ref=index.at[0], dst_ref=index.at[d], send_sem=idx_s.at[0], recv_sem=idx_r.at[d - 1],
            device_id={**peer(d), "tensor": mine - back}, device_id_type=MESH,
        )

    send_rows = to_peers(lambda d: row_out.at[d], row_in, row_s, row_r)
    send_back = [
        pltpu.make_async_remote_copy(
            src_ref=row_send.at[d], dst_ref=row_back.at[d], send_sem=back_s.at[0],
            recv_sem=back_r.at[0], device_id=peer(replicas - d), device_id_type=MESH,
        )
        for d in range(1, replicas)
    ]
    send_tm = to_sides(rank_m, tm_s, tm_r)
    def stay_to(h):
        return pltpu.make_async_remote_copy(
            src_ref=stay_in.at[0], dst_ref=stay_in.at[lax.rem(h - me + replicas, replicas)], send_sem=st_s.at[0],
            recv_sem=st_r.at[0], device_id={"replica": h}, device_id_type=MESH,
        )

    send_down = pltpu.make_async_remote_copy(
        src_ref=hot_down.at[me - base], dst_ref=hot_down.at[me - base], send_sem=hd_s.at[0],
        recv_sem=hd_r.at[0], device_id={"replica": head}, device_id_type=MESH,
    )

    def ranks_to(d, t):
        side_slot = jnp.where(lower, 0, tensors) + t
        return pltpu.make_async_remote_copy(
            src_ref=rank_out.at[d], dst_ref=rank_s.at[side_slot], send_sem=rs_s.at[t],
            recv_sem=rs_r.at[0], device_id={"replica": lax.rem(me - d + replicas, replicas), **side(t)},
            device_id_type=MESH,
        )

    def up_to(d, source):
        return pltpu.make_async_remote_copy(
            src_ref=source, dst_ref=hot_up.at[d], send_sem=hu_s.at[0],
            recv_sem=hu_r.at[0], device_id=peer(d), device_id_type=MESH,
        )

    def start_if(flag, copy):
        @pl.when(flag)
        def _():
            copy.start()

    def sent_if(flag, copy):
        @pl.when(flag)
        def _():
            copy.wait_send()

    load_q.wait()
    for h in range(heads):
        q_rows[pl.ds(h, slots, stride=heads), :] = q_in[:, h * HEAD_DIM:(h + 1) * HEAD_DIM].astype(F32)

    head_row = lax.broadcasted_iota(jnp.int32, (heads, 1), 0) // size
    position = lax.broadcasted_iota(jnp.int32, (1, context), 1)
    scale = 1.0 / math.sqrt(HEAD_DIM)

    def attend(requests):
        requests = list(requests)
        scores = []
        for n in requests:
            q = q_rows[n * heads:(n + 1) * heads, :]
            wide = jnp.concatenate(
                [jnp.where(head_row == g, q, 0.0) for g in range(key_heads)], axis=1
            ).astype(BF16)
            scores.append(jnp.where(position < lengths[n], dot_nt(wide, kv[0, n]) * scale, -jnp.inf))
        scores = jnp.concatenate(scores, axis=0)
        peak = jnp.max(scores, axis=-1, keepdims=True)
        raised = jnp.exp(scores - peak)
        weights = (raised / jnp.sum(raised, axis=-1, keepdims=True)).astype(BF16)
        for i, n in enumerate(requests):
            mixed = dot_nn(weights[i * heads:(i + 1) * heads, :], kv[1, n])
            out = mixed[:, :HEAD_DIM]
            for g in range(1, key_heads):
                out = jnp.where(head_row == g, mixed[:, g * HEAD_DIM:(g + 1) * HEAD_DIM], out)
            o_rows[n * heads:(n + 1) * heads, :] = out

    def gather_rows(first, number):
        return jnp.concatenate(
            [o_rows[pl.ds(first * heads + h, number, stride=heads), :] for h in range(heads)], axis=1
        )

    load_i.wait()
    load_n.wait()
    load_l.wait()
    stay_row = lax.broadcasted_iota(jnp.int32, (STAY, 1), 0)
    stay_home = jnp.zeros((STAY, 1), jnp.int32)
    for i in range(STAY):
        stay_home = jnp.where(stay_row == i, index[0, i] // count, stay_home)
    move_rel = [lax.rem(index[0, STAY + j] // count - me + replicas, replicas) for j in range(moving)]

    load_m.wait()
    attend(range(STAY, slots))
    moved = gather_rows(STAY, moving).astype(BF16)
    attention[STAY:slots, :] = moved
    moved = moved.astype(F32)
    replica_row = lax.broadcasted_iota(jnp.int32, (replicas, 1), 0)
    picked = jnp.zeros((replicas, cols), F32)
    for j in range(moving):
        picked = jnp.where(replica_row == move_rel[j], moved[j:j + 1, :], picked)
    row_in[0] = picked[0:1, :]
    for d in range(1, replicas):
        row_out[d] = picked[d:d + 1, :]

    def homed(slot, slot_range):
        best = jnp.int32(-1)
        for i in slot_range:
            local = index[slot, i] - me * count
            best = jnp.maximum(best, jnp.where((local >= 0) & (local < count), local, -1))
        return best

    def attend_group(g):
        loads[g].wait()
        attend(range(g * GROUP, (g + 1) * GROUP))

    def stage(k):
        for slot, flag in ((k, me >= k), (replicas - k, me + k <= last)):
            @pl.when(flag)
            def _():
                index_to(slot, 0).wait_recv()
                hot[0] = jnp.maximum(hot[0], homed(slot, range(STAY)))
        out_up[k - 1] = up_v[jnp.maximum(hot[0], 0)]
        other = jnp.where(lower, half, half - 1)
        start_if(leads & (me + k <= last) & (me + k != other), up_to(k, out_up.at[k - 1]))
        start_if(leads & (me >= k) & (me - k != other), up_to(replicas - k, out_up.at[k - 1]))

    for g in range(EARLY):
        attend_group(g)
    pl.semaphore_wait(barrier, jnp.where(odd, 2 * replicas + tensors - 3, replicas + tensors - 2))

    for d in range(1, replicas):
        start_if(odd, index_to(d, 1))
        start_if(odd, index_to(d, 0))
    for copy in send_rows:
        copy.start()
    hot[0] = homed(0, range(STAY))
    for g in range(EARLY, groups):
        attend_group(g)
    stay = jnp.where(stay_row < live[0], gather_rows(0, STAY), 0.0).astype(BF16)
    attention[0:STAY, :] = stay
    stay_in[0] = stay
    for h in (half - 1, half):
        start_if(me != h, stay_to(h))
    load_d.wait()
    load_u.wait()
    for k in range(1, replicas):
        stage(k)
    chosen = jnp.maximum(hot[0], 0)
    hot_down[me - base] = down_v[chosen]
    hot_up[0] = up_v[chosen]
    start_if(jnp.logical_not(leads), send_down)
    near = lax.rem(head - me + replicas, replicas)
    for step in range(1, replicas):
        far = replicas - step
        start_if(jnp.logical_not(leads) & lower & (me + far <= last) & (far != near), up_to(far, hot_up.at[0]))
        back_by = replicas - far
        start_if(jnp.logical_not(leads | lower) & (me >= far) & (back_by != near), up_to(back_by, hot_up.at[0]))
    for step in range(1, half):
        start_if(jnp.logical_not(leads) & lower & (me >= step), up_to(replicas - step, hot_up.at[0]))
        start_if(jnp.logical_not(leads | lower) & (me + step <= last), up_to(step, hot_up.at[0]))

    asked = jnp.full((replicas, 1), -1, jnp.int32)
    for d in range(replicas):
        asked = jnp.where(replica_row == d, homed(d, range(STAY, slots)), asked)
    drain(row_in.at[pl.ds(1, last)], row_r)
    rows = jnp.concatenate([row_in[d] for d in range(replicas)], axis=0).astype(BF16)
    partial = dot_nt(rows, down_v[...].reshape(count * rank, cols))
    owner = lax.broadcasted_iota(jnp.int32, partial.shape, 1) // rank
    rank_m[0] = jnp.where(owner == asked, partial, 0.0)
    for copy in send_tm:
        copy.start()

    homes = []
    for d in range(replicas):
        home = jnp.zeros((STAY, 1), jnp.int32)
        for i in range(STAY):
            home = jnp.where(stay_row == i, index[d, i] // count, home)
        homes.append(home)
    homes = jnp.concatenate(homes, axis=0) - base
    drain(rank_m.at[pl.ds(1, tensors - 1)], tm_r)
    total = rank_m[0]
    for d in range(1, tensors):
        total = total + rank_m[d]
    made = widen(total, up_v[...].reshape(count * rank, cols)).astype(BF16).astype(F32)
    row_back[0] = made[0:1, :]
    for d in range(1, replicas):
        row_send[d] = made[d:d + 1, :]
    for copy in send_back:
        copy.start()
    for d in range(1, replicas):
        start_if(jnp.logical_not(leads) & (near == d), up_to(d, hot_up.at[0]))

    part = half * rank
    lines = STAY // 2

    @pl.when(leads)
    def _():
        drain(stay_in.at[pl.ds(1, last)], st_r)
        if half > 1:
            drain(hot_down.at[pl.ds(1, half - 1)], hd_r)
        partial = dot_nt(stay_in[...].reshape(replicas * STAY, cols), hot_down[...].reshape(part, cols))
        owner = lax.broadcasted_iota(jnp.int32, partial.shape, 1) // rank
        partial = jnp.where(owner == homes, partial, 0.0)
        for d in range(replicas):
            block = partial[d * STAY:(d + 1) * STAY]
            rank_out[d] = jnp.concatenate([block[:lines], block[lines:]], axis=1)
        rank_s[jnp.where(lower, 0, tensors)] = rank_out[0]
        for d in range(replicas):
            for t in range(tensors):
                if d or t:
                    ranks_to(d, t).start()
        start_if(lower, up_to(1, hot_up.at[0]))
        start_if(jnp.logical_not(lower), up_to(last, hot_up.at[0]))

    drain(row_back.at[pl.ds(1, last)], back_r)
    back = jnp.concatenate([row_back[d] for d in range(replicas)], axis=0)
    adapted[STAY:slots, :] = jnp.concatenate(
        [
            jnp.sum(jnp.where(replica_row == move_rel[j], back, 0.0), axis=0, keepdims=True)
            for j in range(moving)
        ],
        axis=0,
    ).astype(BF16)

    @pl.when(leads)
    def _():
        drain(rank_s.at[pl.ds(1, 2 * tensors - 1)], rs_r)

    @pl.when(jnp.logical_not(leads))
    def _():
        drain(rank_s, rs_r)

    totals = []
    for side_slot in (0, tensors):
        total = rank_s[side_slot]
        for d in range(1, tensors):
            total = total + rank_s[side_slot + d]
        totals.append(jnp.concatenate([total[:, :part], total[:, part:]], axis=0))
    total = jnp.concatenate(totals, axis=1)
    drain(hot_up.at[pl.ds(1, last)], hu_r)
    ups = jnp.concatenate([hot_up[lax.rem(me - h + replicas, replicas)] for h in range(replicas)], axis=0)
    adapted[0:STAY, :] = widen(total, ups).astype(BF16)

    @pl.when(odd)
    def _():
        drain(index.at[pl.ds(1, last)], idx_s)
        drain(index.at[pl.ds(1, last)], idx_s)

    drain(row_out.at[pl.ds(1, last)], row_s)
    drain(row_send.at[pl.ds(1, last)], back_s)
    drain(rank_m.at[pl.ds(1, tensors - 1)], tm_s)
    drain(hot_up.at[pl.ds(1, last)], hu_s)

    @pl.when(leads)
    def _():
        drain(stay_in.at[0], st_s)
        drain(rank_out.at[pl.ds(1, last)], rs_s.at[pl.ds(0, 1)])
        for t in range(1, tensors):
            drain(rank_out, rs_s.at[pl.ds(t, 1)])

    @pl.when(jnp.logical_not(leads))
    def _():
        drain(stay_in.at[pl.ds(0, 2)], st_s)
        drain(hot_down.at[0], hd_s)


def hand_over(attention, adapted, attention_out, adapted_out, sem):
    first = pltpu.make_async_copy(attention, attention_out, sem.at[0])
    second = pltpu.make_async_copy(adapted, adapted_out, sem.at[1])
    first.start()
    second.start()
    first.wait()
    second.wait()


def on_device(replicas, tensors, queries, past_cache, lengths, live_counts, adapter_index, adapter_down, adapter_up):
    slots, cols = queries.shape
    count, rank = adapter_down.shape[0], adapter_down.shape[1]
    heads = cols // HEAD_DIM
    out = jax.ShapeDtypeStruct((slots, cols), BF16)
    held = pltpu.VMEM((slots, cols), BF16)
    anywhere = pl.BlockSpec(memory_space=pl.ANY)
    vmem = pl.BlockSpec(memory_space=pltpu.VMEM)
    dma = pltpu.SemaphoreType.DMA
    rep = dma((replicas - 1,))
    one = dma((1,))
    ten = dma((tensors,))
    half = replicas // 2
    scratch = [
        pltpu.SMEM((slots,), jnp.int32),
        pltpu.SMEM((1,), jnp.int32),
        pltpu.SMEM((replicas, slots), jnp.int32),
        pltpu.SMEM((1,), jnp.int32),
        pltpu.VMEM((slots, cols), BF16),
        pltpu.VMEM(past_cache.shape, BF16),
        pltpu.VMEM((2, *adapter_down.shape), BF16),
        pltpu.VMEM((slots * heads, HEAD_DIM), F32),
        pltpu.VMEM((slots * heads, HEAD_DIM), F32),
        pltpu.VMEM((replicas, 1, cols), F32),
        pltpu.VMEM((replicas, 1, cols), F32),
        pltpu.VMEM((replicas, 1, cols), F32),
        pltpu.VMEM((replicas, 1, cols), F32),
        pltpu.VMEM((replicas - 1, rank, cols), BF16),
        pltpu.VMEM((half, rank, cols), BF16),
        pltpu.VMEM((replicas, rank, cols), BF16),
        pltpu.VMEM((replicas, STAY, cols), BF16),
        pltpu.VMEM((tensors, replicas, count * rank), F32),
        pltpu.VMEM((replicas, STAY // 2, replicas * rank), F32),
        pltpu.VMEM((2 * tensors, STAY // 2, replicas * rank), F32),
        dma((7,)),
        dma((STAY // GROUP,)),
        one, rep, one, one, one, one, one, one, one, one, one, one, one, one, ten, one,
    ]
    results = pl.pallas_call(
        functools.partial(kernel, replicas, tensors),
        out_shape=(held, held),
        in_specs=[anywhere] * 7,
        out_specs=(vmem, vmem),
        scratch_shapes=scratch,
        compiler_params=pltpu.CompilerParams(collective_id=0, has_side_effects=True, vmem_limit_bytes=LIMIT),
    )(lengths, live_counts, adapter_index, queries, past_cache, adapter_down, adapter_up)
    return pl.pallas_call(
        hand_over,
        out_shape=(out, out),
        in_specs=[vmem, vmem],
        out_specs=(anywhere, anywhere),
        scratch_shapes=[dma((2,))],
        compiler_params=pltpu.CompilerParams(vmem_limit_bytes=4 * 1024 * 1024),
    )(*results)


def solution(mesh):
    in_specs = (
        P(("groups", "replica"), "tensor"),
        P(None, ("groups", "replica"), None, "tensor"),
        P(("groups", "replica")),
        P(("groups", "replica")),
        P(("groups", "replica")),
        P("replica", None, "tensor"),
        P("replica", None, "tensor"),
    )
    out_specs = (P(("groups", "replica"), "tensor"), P(("groups", "replica"), "tensor"))
    body = functools.partial(on_device, mesh.shape["replica"], mesh.shape["tensor"])
    return jax.shard_map(body, mesh=mesh, in_specs=in_specs, out_specs=out_specs, check_vma=False)
```
